32 devices in a mesh: groups: 2 (over x), seq: 8 (over z, y), exp: 2 (over core).
Axes of the slice: x: 2, y: 2, z: 4, core: 2. Of those that a mesh axis runs over, the one named last changes fastest.
Arguments:
- stream: bfloat16 [2048, 2048], P(('groups', 'seq', 'exp')), parts along dimension 0, may hold values from -5 to 5
- queries: bfloat16 [2048, 4096], P(('groups', 'seq'), 'exp'), parts along dimension 0, may hold values from -131 to 131
- key_rows: bfloat16 [2048, 512], P(('groups', 'seq'), 'exp'), parts along dimension 0, may hold values from -4 to 4
- value_rows: bfloat16 [2048, 512], P(('groups', 'seq'), 'exp'), parts along dimension 0, may hold values from -4 to 4
- out_weight: bfloat16 [2048, 4096], P('seq', 'exp'), may hold values from -0.375 to 0.375
- norm_gain: float32 [2048], replicated, may hold values from 0.1 to 1.9
- expert_ids: int32 [2048, 8], P(('groups', 'seq', 'exp')), parts along dimension 0, may hold values from 0 to 63, all different within a row; in each aligned block of 64 rows (0 to 63, 64 to 127, ...) at most 12 rows name the same one
- gate_weights: float32 [2048, 8], P(('groups', 'seq', 'exp')), parts along dimension 0, may hold values from 0.05 to 0.5
- expert_in: bfloat16 [64, 2048, 1536], P(('seq', 'exp')), may hold values from -0.125 to 0.125
- expert_out: bfloat16 [64, 768, 2048], P(('seq', 'exp')), may hold values from -0.21875 to 0.21875
Outputs:
- layer_out: bfloat16 [2048, 2048], P(('groups', 'seq', 'exp')), parts along dimension 0
The draws below stay inside these ranges and needn't reach their ends.
There are 2 independent parts, one for each index of `groups`. The reference program is written for one: setup_inputs(seed, part) draws one part's arguments, and reference() takes and returns one part's arrays. A program takes and returns all parts, laid end to end along the dimension named above; an argument that names none is the same for every part. Nothing has to cross between parts.
Inputs may be any that keep to these rules, and one draw needn't show every extreme that they name: `expert_ids`: each row names 8 different experts. Among the 64 rows of one device (aligned blocks of rows), no expert is named more than 12 times, a bound that some block reaches.
All inputs are finite; a program needn't handle non-finite values.
Results may differ from the reference program's by a relative error of at most 0.0095.
Values may be sent and summed in bfloat16 or wider, within the bound.
A program may use at most 128 MiB of HBM per device.

```python
import math
import jax
import jax.numpy as jnp
import numpy as np
from jax import lax

D = 2048
H = 32
KVH = 4
HD = 128
F = 768
EXPERTS = 64
TOPK = 8
CAP = 12
SPAN = 128
SEQLEN = 1024
MROWS = 64


def draw_pair(key):
    base = jax.random.fold_in(key, 7101)
    key_part, query_part = jax.random.split(base, 2)
    per_group = H // KVH
    keyed = jnp.clip(jax.random.normal(key_part, (SEQLEN, KVH, HD), jnp.float32), -3.5, 3.5)
    queried = jnp.clip(jax.random.normal(query_part, (SEQLEN, KVH, per_group, HD), jnp.float32), -3.5, 3.5)
    return (queried, keyed)


def draw_queries(key, part):
    queried, keyed = draw_pair(key)
    return queried.reshape(SEQLEN, H * HD).astype(jnp.bfloat16)


def draw_key_rows(key, part):
    queried, keyed = draw_pair(key)
    return keyed.reshape(SEQLEN, KVH * HD).astype(jnp.bfloat16)


def steps_of(key, shape, shards, least, high):
    def one(axis_at, parts):
        heights = jax.random.uniform(jax.random.fold_in(jax.random.fold_in(key, 6), axis_at), (parts,), jnp.float32, least / len(shards), high / len(shards))
        return jnp.repeat(jnp.exp(heights), shape[axis_at] // parts).reshape((-1,) + (1,) * (len(shape) - axis_at - 1))

    loudness = one(*shards[0])
    for cut in shards[1:]:
        loudness = loudness * one(*cut)
    return loudness


def assign_block(stream_key, own, number, rows, count, top, most, slope):
    sequence = jax.random.permutation(stream_key, count)
    packed, common = shares(count, rows * top, most, slope, True), shares(count, rows * top, most, slope, False)
    places = jnp.arange(count)

    def named(tallies, rotation):
        used = int((tallies > 0).sum())
        fixed = max(1, used // 4)
        passed = fixed + (places - fixed + rotation * (used - fixed)) % max(1, count - fixed)
        return jnp.zeros((count,), jnp.int32).at[sequence[jnp.where(places < fixed, places, passed)]].set(jnp.asarray(tallies, jnp.int32))

    tallies = jnp.where(number % 4 == 0, named(packed, number // 4), named(common, number - number // 4 - 1))
    mixed = jax.random.permutation(jax.random.fold_in(own, 3), count)
    giver, receiver = mixed[0:count // 2 * 2:2], mixed[1:count // 2 * 2:2]
    margin = jnp.minimum(tallies[giver] - 1, most - tallies[receiver]) // 2
    margin = jnp.where((giver == sequence[0]) | (receiver == sequence[0]) | (tallies[receiver] == 0), 0, jnp.maximum(margin, 0))
    passed = jax.random.randint(jax.random.fold_in(own, 4), (count // 2,), 0, 1 << 20) % (margin + 1)
    tallies = tallies.at[giver].add(-passed).at[receiver].add(passed)
    members = jnp.searchsorted(jnp.cumsum(tallies), jnp.arange(rows * top), side="right").astype(jnp.int32)
    listing = members.reshape(top, rows).T
    listing = listing[jax.random.permutation(jax.random.fold_in(own, 1), rows)]
    rotation = jax.random.randint(jax.random.fold_in(own, 2), (rows, 1), 0, top)
    return jnp.take_along_axis(listing, (jnp.arange(top)[None, :] + rotation) % top, axis=1)


def shares(count, total, most, lean, full):
    loads = [(1 << 20) // math.isqrt(grade ** lean) + 1 for grade in range(1, count + 1)]
    largest = most if full else min(most, max(-(-total // count), total * loads[0] // sum(loads)))
    least = 1 if total - largest >= count - 1 else 0
    holding, rest = [largest] + [least] * (count - 1), total - largest - least * (count - 1)
    while rest > 0:
        movable = [i for i in range(1, count) if holding[i] < largest] or [i for i in range(1, count) if holding[i] < most]
        pool, remaining = sum([loads[i] for i in movable]), rest
        for i in movable:
            more = min(most - holding[i], max(1, remaining * loads[i] // pool), rest)
            holding[i] = holding[i] + more
            rest = rest - more
    return np.array(holding)


def normal_values(rng, shape, deviation, most, pieces=(), held_as=jnp.bfloat16):
    result = deviation * jax.random.normal(rng, shape, jnp.float32)
    if pieces:
        result = result * steps_of(rng, shape, pieces, -0.22, 0.18)
    return jnp.clip(result, -most, most).astype(held_as)


def setup_inputs(seed: int = 0, part: int = 0) -> dict:
    key_list = jax.random.split(jax.random.key(seed), 11)
    own_keys = jax.random.split(jax.random.fold_in(key_list[10], part), 11)
    stream = normal_values(own_keys[0], (SEQLEN, D), 1.0, 5.0, ((0, 16),))
    queries = draw_queries(jax.random.fold_in(jax.random.fold_in(key_list[10], part), 71), part)
    key_rows = draw_key_rows(jax.random.fold_in(jax.random.fold_in(key_list[10], part), 71), part)
    value_rows = normal_values(own_keys[3], (SEQLEN, KVH * HD), 1.0, 4.0, ((0, 8), (1, 2)))
    out_weight = normal_values(key_list[4], (D, H * HD), (H * HD // 16) ** -0.5, 0.375, ((0, 8), (1, 2)))
    norm_gain = jnp.clip(1.0 + 0.18 * jax.random.normal(key_list[5], (D,), jnp.float32), 0.1, 1.9)
    expert_ids_keys = jax.random.split(jax.random.fold_in(own_keys[6], 1), SEQLEN // MROWS)
    expert_ids_turns = jax.random.permutation(jax.random.fold_in(own_keys[6], 3), SEQLEN // MROWS)
    expert_ids = jax.vmap(lambda own, number: assign_block(jax.random.fold_in(own_keys[6], 2), own, number, MROWS, EXPERTS, TOPK, CAP, 2))(expert_ids_keys, expert_ids_turns).reshape((SEQLEN, TOPK))
    gate_weights = jnp.clip(jnp.exp(math.log(0.5) - 2.3025851 * jax.random.uniform(own_keys[7], (SEQLEN, TOPK), jnp.float32) ** steps_of(own_keys[7], (SEQLEN, TOPK), ((0, 16),), -0.2, 0.2)), 0.05, 0.5)
    expert_in = normal_values(key_list[8], (EXPERTS, D, 2 * F), D ** -0.5, 0.125, ((0, 16),))
    expert_out = normal_values(key_list[9], (EXPERTS, F, D), F ** -0.5, 0.21875, ((0, 16),))
    return {"stream": stream, "queries": queries, "key_rows": key_rows, "value_rows": value_rows, "out_weight": out_weight, "norm_gain": norm_gain, "expert_ids": expert_ids, "gate_weights": gate_weights, "expert_in": expert_in, "expert_out": expert_out}


def attend_block(query_block, block_start, key_rows, value_rows):
    rows = query_block.shape[0]
    per_group = H // KVH
    grouped = query_block.reshape(rows, KVH, per_group, HD).astype(jnp.float32)
    keyed = key_rows.reshape(-1, KVH, HD).astype(jnp.float32)
    valued = value_rows.reshape(-1, KVH, HD).astype(jnp.float32)
    scores = jnp.einsum('tghd,sgd->gths', grouped, keyed) / jnp.sqrt(jnp.float32(HD))
    query_pos = block_start + jnp.arange(rows, dtype=jnp.int32)
    key_pos = jnp.arange(keyed.shape[0], dtype=jnp.int32)
    allowed = (key_pos[None, :] <= query_pos[:, None])[None, :, None, :]
    scores = jnp.where(allowed, scores, jnp.float32(-1e+30))
    largest = lax.optimization_barrier(jnp.max(scores, axis=-1, keepdims=True))
    exps = jnp.where(allowed, jnp.exp(scores - largest), jnp.float32(0.0))
    total = lax.optimization_barrier(jnp.sum(exps, axis=-1))
    probs = exps.astype(jnp.bfloat16)
    summed = jnp.einsum('gths,sgd->gthd', probs.astype(jnp.float32), valued)
    context = summed / total[..., None]
    return context.transpose(1, 0, 2, 3).reshape(rows, H * HD).astype(jnp.bfloat16)

def reference(stream, queries, key_rows, value_rows, out_weight, norm_gain, expert_ids, gate_weights, expert_in, expert_out):
    block_count = SEQLEN // SPAN
    blocks = queries.reshape(block_count, SPAN, H * HD)
    starts = jnp.arange(block_count, dtype=jnp.int32) * SPAN
    context = lax.map(lambda pair: attend_block(pair[0], pair[1], key_rows, value_rows), (blocks, starts))
    context = context.reshape(SEQLEN, H * HD)
    attn_out = jnp.dot(context, out_weight.T, preferred_element_type=jnp.float32)
    mixed = stream.astype(jnp.float32) + attn_out
    normed = (mixed * lax.rsqrt(lax.optimization_barrier(jnp.mean(mixed * mixed, axis=-1, keepdims=True)) + 1e-06) * norm_gain).astype(jnp.bfloat16)
    group_count = SEQLEN // MROWS
    assigned = MROWS * TOPK
    flat_ids = expert_ids.reshape(group_count, assigned)
    onehot = (flat_ids[..., None] == jnp.arange(EXPERTS, dtype=jnp.int32)[None, None, :]).astype(jnp.int32)
    earlier = jnp.cumsum(onehot, axis=1) - onehot
    slots = lax.optimization_barrier(jnp.sum(earlier * onehot, axis=-1)).astype(jnp.int32)
    group_index = jnp.arange(group_count, dtype=jnp.int32)[:, None]
    token_index = group_index * MROWS + jnp.arange(assigned, dtype=jnp.int32)[None, :] // TOPK
    position = (flat_ids * (group_count * CAP) + group_index * CAP + slots).astype(jnp.int32).reshape(-1)
    table = jnp.zeros((EXPERTS * group_count * CAP,), jnp.int32).at[position].set(token_index.reshape(-1).astype(jnp.int32))

    def run_expert(pack):
        rows_index, first, second = pack
        inputs = normed[rows_index]
        gate_up = jnp.dot(inputs, first, preferred_element_type=jnp.float32)
        act = (jax.nn.silu(gate_up[:, :F]) * gate_up[:, F:]).astype(jnp.bfloat16)
        return jnp.dot(act, second, preferred_element_type=jnp.float32).astype(jnp.bfloat16)
    results = lax.map(run_expert, (table.reshape(EXPERTS, group_count * CAP), expert_in, expert_out))
    picked = results.reshape(-1, D)[position].reshape(SEQLEN, TOPK, D)
    combined = lax.optimization_barrier(jnp.sum(gate_weights[..., None] * picked.astype(jnp.float32), axis=1))
    return (mixed + combined).astype(jnp.bfloat16)
```

```python
import functools

import jax
import jax.numpy as jnp
from jax import lax
from jax.experimental import pallas as pl
from jax.experimental.pallas import tpu as pltpu
from jax.sharding import PartitionSpec as P

HD = 128
EXPERTS = 64
CAP = 12
LOW = 2
PARTS = 2
VMEM_LIMIT = 60 * 1024 * 1024
neg_large = -1e30


def split_position():
    seq = lax.axis_index("seq")
    return seq // LOW, seq % LOW, lax.axis_index("exp")


def line_barrier(high, h, l, e):
    barrier = pltpu.get_barrier_semaphore()

    def greet(target):
        pl.semaphore_signal(barrier, inc=1, device_id=target, device_id_type=pl.DeviceIdType.MESH)

    @pl.when(h + 1 < high)
    def _():
        greet({"seq": (h + 1) * LOW + l})

    @pl.when(h > 0)
    def _():
        greet({"seq": (h - 1) * LOW + l})

    greet({"seq": h * LOW + 1 - l})
    greet({"exp": 1 - e})

    ends = jnp.where(h + 1 < high, 1, 0) + jnp.where(h > 0, 1, 0)
    pl.semaphore_wait(barrier, ends + 2)


def gather_steps(high, outs, cross, parts, recv, send, h, l, e):
    count = len(outs)

    def slot(a, h0, l0, e0, c):
        rows = outs[a].shape[-2] // parts[a]
        at = (h0, l0, e0) if cross[a] else (h0, l0)
        return outs[a].at[at + (pl.ds(c * rows, rows),)]

    def copy(a, h0, l0, e0, c, way):
        target = (
            {"seq": (h + 1) * LOW + l},
            {"seq": (h - 1) * LOW + l},
            {"seq": h * LOW + 1 - l},
            {"exp": 1 - e},
        )[way]
        ref = slot(a, h0, l0, e0, c)
        return pltpu.make_async_remote_copy(
            src_ref=ref,
            dst_ref=ref,
            send_sem=send[a].at[way, h0, l0, c],
            recv_sem=recv[a].at[h0, l0, e0, c],
            device_id=target,
            device_id_type=pl.DeviceIdType.MESH,
        )

    def pass_on(a, h0, c, right, left):
        if right:
            @pl.when(h + 1 < high)
            def _():
                copy(a, h0, l, e, c, 0).start()
        if left:
            @pl.when(h > 0)
            def _():
                copy(a, h0, l, e, c, 1).start()
        copy(a, h0, l, e, c, 2).start()
        if cross[a]:
            copy(a, h0, l, e, c, 3).start()

    def from_across(a, h0, c):
        copy(a, h0, 1 - l, e, c, 2).wait_recv()
        if cross[a]:
            copy(a, h0, 1 - l, e, c, 3).start()

    for a in range(count):
        for c in range(parts[a]):
            pass_on(a, h, c, True, True)
    for t in range(1, high + 1):
        if t < high:
            for a in range(count):
                for c in range(parts[a]):
                    @pl.when(h - t >= 0)
                    def _():
                        copy(a, h - t, l, e, c, 0).wait_recv()
                        pass_on(a, h - t, c, True, False)

                    @pl.when(h + t < high)
                    def _():
                        copy(a, h + t, l, e, c, 1).wait_recv()
                        pass_on(a, h + t, c, False, True)
        for a in range(count):
            for c in range(parts[a]):
                if t == 1:
                    from_across(a, h, c)
                else:
                    @pl.when(h - t + 1 >= 0)
                    def _():
                        from_across(a, h - t + 1, c)

                    @pl.when(h + t - 1 < high)
                    def _():
                        from_across(a, h + t - 1, c)
    for a in range(count):
        for c in range(parts[a]):
            for h0 in range(high):
                if cross[a]:
                    for l0 in range(LOW):
                        copy(a, h0, l0, 1 - e, c, 3).wait_recv()
                        copy(a, h0, l0, e, c, 3).wait_send()
                copy(a, h0, l, e, c, 2).wait_send()

                @pl.when((h + 1 < high) & (h0 <= h))
                def _():
                    copy(a, h0, l, e, c, 0).wait_send()

                @pl.when((h > 0) & (h0 >= h))
                def _():
                    copy(a, h0, l, e, c, 1).wait_send()


def gather_kernel(high, cross, parts, *refs):
    count = len(cross)
    ins, outs = refs[:count], refs[count : 2 * count]
    recv = refs[2 * count : 3 * count]
    send = refs[3 * count : 4 * count]
    local = refs[4 * count]
    h, l, e = split_position()
    copies = []
    for a in range(count):
        at = (h, l, e) if cross[a] else (h, l)
        copies.append(pltpu.make_async_copy(ins[a], outs[a].at[at], local.at[a]))
        copies[-1].start()
    line_barrier(high, h, l, e)
    for one in copies:
        one.wait()
    gather_steps(high, outs, cross, parts, recv, send, h, l, e)


def gather(arrays, cross, parts, high, collective_id):
    count = len(arrays)
    exp_count = 2
    outs = []
    for array, both in zip(arrays, cross):
        lead = (high, LOW, exp_count) if both else (high, LOW)
        outs.append(jax.ShapeDtypeStruct(lead + array.shape, array.dtype))
    whole = pl.BlockSpec(memory_space=pltpu.VMEM)
    return pl.pallas_call(
        functools.partial(gather_kernel, high, cross, parts),
        out_shape=tuple(outs),
        in_specs=[whole] * count,
        out_specs=tuple([whole] * count),
        scratch_shapes=[pltpu.SemaphoreType.DMA((high, LOW, exp_count, p)) for p in parts]
        + [pltpu.SemaphoreType.DMA((4, high, LOW, p)) for p in parts]
        + [pltpu.SemaphoreType.DMA((count,))],
        compiler_params=pltpu.CompilerParams(
            collective_id=collective_id, has_side_effects=True, vmem_limit_bytes=VMEM_LIMIT
        ),
        name="gather" + str(collective_id),
    )(*arrays)


def exchange_kernel(
    seq_count, part_ref, stream_ref, gain_ref, mixed_ref, normed_ref, mine, ready, landed, sem_a, sem_b, sem_c, sem_d
):
    me = lax.axis_index("seq")
    e = lax.axis_index("exp")
    features = part_ref.shape[-1]
    barrier = pltpu.get_barrier_semaphore()
    mesh_id = pl.DeviceIdType.MESH
    pl.semaphore_signal(barrier, inc=1, device_id={"exp": 1 - e}, device_id_type=mesh_id)
    for d in range(1, seq_count):
        pl.semaphore_signal(
            barrier, inc=1, device_id={"seq": (me + d) % seq_count}, device_id_type=mesh_id
        )
    pl.semaphore_wait(barrier, seq_count)

    def over(s):
        return pltpu.make_async_remote_copy(
            src_ref=part_ref.at[s, 1 - e],
            dst_ref=mine.at[s],
            send_sem=sem_a.at[s],
            recv_sem=sem_b.at[s],
            device_id={"exp": 1 - e},
            device_id_type=mesh_id,
        )

    def away(d, source):
        return pltpu.make_async_remote_copy(
            src_ref=ready.at[(me + d) % seq_count],
            dst_ref=landed.at[source],
            send_sem=sem_c.at[d],
            recv_sem=sem_d.at[source],
            device_id={"seq": (me + d) % seq_count},
            device_id_type=mesh_id,
        )

    order = list(range(1, seq_count)) + [0]
    for d in order:
        over((me + d) % seq_count).start()
    for d in order:
        s = (me + d) % seq_count
        over(s).wait_recv()
        total = part_ref[s, e].astype(jnp.float32) + mine[s].astype(jnp.float32)
        ready[s] = total.astype(ready.dtype)
        if d:
            away(d, me).start()
    landed[me] = ready[me]
    for d in range(1, seq_count):
        away(d, (me + seq_count - d) % seq_count).wait_recv()
    squares = None
    for s in range(seq_count):
        columns = pl.ds(s * features, features)
        value = stream_ref[:, columns].astype(jnp.float32) + landed[s].astype(jnp.float32)
        mixed_ref[:, columns] = value
        term = jnp.sum(value * value, axis=-1, keepdims=True)
        squares = term if squares is None else squares + term
    width = seq_count * features
    factor = lax.rsqrt(squares / width + 1e-06)
    for s in range(seq_count):
        columns = pl.ds(s * features, features)
        normed_ref[:, columns] = (mixed_ref[:, columns] * factor * gain_ref[:, columns]).astype(
            normed_ref.dtype
        )
    for d in range(seq_count):
        over(d).wait_send()
    for d in range(1, seq_count):
        away(d, me).wait_send()


def exchange(part, stream, gain):
    seq_count = part.shape[0]
    rows, features = part.shape[2:]
    whole = pl.BlockSpec(memory_space=pltpu.VMEM)
    return pl.pallas_call(
        functools.partial(exchange_kernel, seq_count),
        out_shape=(
            jax.ShapeDtypeStruct(stream.shape, jnp.float32),
            jax.ShapeDtypeStruct(stream.shape, jnp.bfloat16),
        ),
        in_specs=[whole] * 3,
        out_specs=(whole, whole),
        scratch_shapes=[pltpu.VMEM((seq_count, rows, features), part.dtype) for _ in range(3)]
        + [pltpu.SemaphoreType.DMA((seq_count,)) for _ in range(4)],
        compiler_params=pltpu.CompilerParams(
            collective_id=3, has_side_effects=True, vmem_limit_bytes=VMEM_LIMIT
        ),
        name="exchange",
    )(part, stream, gain)


def scatter_kernel(
    high, parts, part_ref, mixed_ref, out_ref, near, sums, across, running, line,
    near_s, near_r, across_s, across_r, line_s, line_r
):
    h, l, e = split_position()
    rows = part_ref.shape[-2] // parts
    mesh_id = pl.DeviceIdType.MESH
    order = []
    for i in range(high):
        order.append(i // 2 if i % 2 == 0 else high - 1 - i // 2)
    line_barrier(high, h, l, e)

    def to_near(h0, l0, c):
        at = pl.ds(c * rows, rows)
        return pltpu.make_async_remote_copy(
            src_ref=part_ref.at[h0, l0, 1 - e, at],
            dst_ref=near.at[h0, l0, at],
            send_sem=near_s.at[h0, l0, c],
            recv_sem=near_r.at[h0, l0, c],
            device_id={"exp": 1 - e},
            device_id_type=mesh_id,
        )

    def to_across(h0, c):
        at = pl.ds(c * rows, rows)
        return pltpu.make_async_remote_copy(
            src_ref=sums.at[h0, at],
            dst_ref=across.at[h0, at],
            send_sem=across_s.at[h0, c],
            recv_sem=across_r.at[h0, c],
            device_id={"seq": h * LOW + 1 - l},
            device_id_type=mesh_id,
        )

    def to_line(way, h0, c):
        at = pl.ds(c * rows, rows)
        return pltpu.make_async_remote_copy(
            src_ref=running.at[h0, at],
            dst_ref=line.at[way, h0, at],
            send_sem=line_s.at[way, h0, c],
            recv_sem=line_r.at[way, h0, c],
            device_id={"seq": (h - 1 + 2 * way) * LOW + l},
            device_id_type=mesh_id,
        )

    pieces = [(h0, c) for h0 in order for c in range(parts)]
    for h0, c in pieces:
        to_near(h0, 1 - l, c).start()
    for h0, c in pieces:
        to_near(h0, l, c).start()
    for h0, c in pieces:
        at = pl.ds(c * rows, rows)
        to_near(h0, 1 - l, c).wait_recv()
        value = part_ref[h0, 1 - l, e, at].astype(jnp.float32) + near[h0, 1 - l, at].astype(jnp.float32)
        sums[h0, at] = value.astype(sums.dtype)
        to_across(h0, c).start()
    for h0, c in pieces:
        at = pl.ds(c * rows, rows)
        to_near(h0, l, c).wait_recv()
        to_across(h0, c).wait_recv()

        def held():
            value = part_ref[h0, l, e, at].astype(jnp.float32) + near[h0, l, at].astype(jnp.float32)
            return value + across[h0, at].astype(jnp.float32)

        @pl.when(h0 < h)
        def _():
            @pl.when(h + 1 < high)
            def _():
                to_line(0, h0, c).wait_recv()
                running[h0, at] = (held() + line[0, h0, at].astype(jnp.float32)).astype(running.dtype)

            @pl.when(h + 1 >= high)
            def _():
                running[h0, at] = held().astype(running.dtype)

            to_line(0, h0, c).start()

        @pl.when(h0 > h)
        def _():
            @pl.when(h > 0)
            def _():
                to_line(1, h0, c).wait_recv()
                running[h0, at] = (held() + line[1, h0, at].astype(jnp.float32)).astype(running.dtype)

            @pl.when(h <= 0)
            def _():
                running[h0, at] = held().astype(running.dtype)

            to_line(1, h0, c).start()
    for c in range(parts):
        at = pl.ds(c * rows, rows)
        value = part_ref[h, l, e, at].astype(jnp.float32) + near[h, l, at].astype(jnp.float32)
        value = value + across[h, at].astype(jnp.float32) + mixed_ref[at, :]
        mixed_ref_sum = value

        @pl.when(h + 1 < high)
        def _():
            to_line(0, h, c).wait_recv()

        @pl.when(h + 1 >= high)
        def _():
            line[0, h, at] = jnp.zeros_like(line[0, h, at])

        @pl.when(h > 0)
        def _():
            to_line(1, h, c).wait_recv()

        @pl.when(h <= 0)
        def _():
            line[1, h, at] = jnp.zeros_like(line[1, h, at])

        value = mixed_ref_sum + line[0, h, at].astype(jnp.float32) + line[1, h, at].astype(jnp.float32)
        out_ref[at, :] = value.astype(out_ref.dtype)
    for h0, c in pieces:
        to_near(h0, l, c).wait_send()
        to_near(h0, 1 - l, c).wait_send()
        to_across(h0, c).wait_send()

        @pl.when(h0 < h)
        def _():
            to_line(0, h0, c).wait_send()

        @pl.when(h0 > h)
        def _():
            to_line(1, h0, c).wait_send()


def scatter(part, mixed, high):
    rows, width = mixed.shape
    parts = PARTS
    whole = pl.BlockSpec(memory_space=pltpu.VMEM)
    kind = part.dtype
    return pl.pallas_call(
        functools.partial(scatter_kernel, high, parts),
        out_shape=jax.ShapeDtypeStruct((rows, width), jnp.bfloat16),
        in_specs=[whole] * 2,
        out_specs=whole,
        scratch_shapes=[
            pltpu.VMEM((high, LOW, rows, width), kind),
            pltpu.VMEM((high, rows, width), kind),
            pltpu.VMEM((high, rows, width), kind),
            pltpu.VMEM((high, rows, width), kind),
            pltpu.VMEM((2, high, rows, width), kind),
        ]
        + [pltpu.SemaphoreType.DMA((high, LOW, parts))] * 2
        + [pltpu.SemaphoreType.DMA((high, parts))] * 2
        + [pltpu.SemaphoreType.DMA((2, high, parts))] * 2,
        compiler_params=pltpu.CompilerParams(
            collective_id=5, has_side_effects=True, vmem_limit_bytes=VMEM_LIMIT
        ),
        name="scatter",
    )(part, mixed)


def attend(queries, keys, values, query_start):
    rows = queries.shape[0]
    groups = keys.shape[1] // HD
    per_group = queries.shape[1] // (groups * HD)
    query_group = queries.reshape(rows, groups, per_group, HD)
    keyed = keys.reshape(-1, groups, HD)
    valued = values.reshape(-1, groups, HD)
    scores = jnp.einsum(
        "tghd,sgd->gths", query_group, keyed, preferred_element_type=jnp.float32
    ) / jnp.sqrt(jnp.float32(HD))
    query_pos = query_start + jnp.arange(rows, dtype=jnp.int32)
    key_pos = jnp.arange(keyed.shape[0], dtype=jnp.int32)
    allowed = (key_pos[None, :] <= query_pos[:, None])[None, :, None, :]
    scores = jnp.where(allowed, scores, neg_large)
    exps = jnp.exp(scores - jnp.max(scores, axis=-1, keepdims=True))
    total = jnp.sum(exps, axis=-1)
    summed = jnp.einsum(
        "gths,sgd->gthd", exps.astype(jnp.bfloat16), valued, preferred_element_type=jnp.float32
    )
    return (summed / total[..., None]).transpose(1, 0, 2, 3).reshape(rows, -1).astype(jnp.bfloat16)


def attend_kernel(query_ref, kv_ref, out_ref):
    blocks, span, double = kv_ref.shape
    half = double // 2
    groups = half // HD
    rows = query_ref.shape[0]
    per_group = query_ref.shape[1] // (groups * HD)
    me = lax.axis_index("seq")
    scale = 1.0 / (HD ** 0.5)
    stacked = per_group * rows
    for g in range(groups):
        q = jnp.concatenate(
            [query_ref[:, pl.ds((g * per_group + i) * HD, HD)] for i in range(per_group)], axis=0
        )

        def piece(b, state, masked):
            largest, total, summed = state
            k = kv_ref[b, :, pl.ds(g * HD, HD)]
            v = kv_ref[b, :, pl.ds(half + g * HD, HD)]
            scores = lax.dot_general(
                q, k, (((1,), (1,)), ((), ())), preferred_element_type=jnp.float32
            ) * scale
            if masked:
                row = lax.broadcasted_iota(jnp.int32, scores.shape, 0) % rows
                column = lax.broadcasted_iota(jnp.int32, scores.shape, 1)
                scores = jnp.where(column <= row, scores, neg_large)
            new = jnp.maximum(largest, jnp.max(scores, axis=-1, keepdims=True))
            rescale = jnp.exp(largest - new)
            exps = jnp.exp(scores - new)
            total = total * rescale + jnp.sum(exps, axis=-1, keepdims=True)
            summed = summed * rescale + jnp.dot(
                exps.astype(jnp.bfloat16), v, preferred_element_type=jnp.float32
            )
            return new, total, summed

        state = (
            jnp.full((stacked, 1), neg_large, jnp.float32),
            jnp.zeros((stacked, 1), jnp.float32),
            jnp.zeros((stacked, HD), jnp.float32),
        )
        state = piece(me, state, True)
        state = lax.fori_loop(0, me, lambda b, s: piece(b, s, False), state)
        result = (state[2] / state[1]).astype(out_ref.dtype)
        for i in range(per_group):
            out_ref[:, pl.ds((g * per_group + i) * HD, HD)] = result[i * rows : (i + 1) * rows]


def attend_fast(queries, kv):
    whole = pl.BlockSpec(memory_space=pltpu.VMEM)
    return pl.pallas_call(
        attend_kernel,
        out_shape=jax.ShapeDtypeStruct(queries.shape, jnp.bfloat16),
        in_specs=[whole] * 2,
        out_specs=whole,
        compiler_params=pltpu.CompilerParams(vmem_limit_bytes=VMEM_LIMIT),
        name="attend",
    )(queries, kv)


def on_device(
    stream,
    queries,
    key_rows,
    value_rows,
    out_weight,
    norm_gain,
    expert_ids,
    gate_weights,
    expert_in,
    expert_out,
):
    seq_count = lax.axis_size("seq")
    exp_count = lax.axis_size("exp")
    high = seq_count // LOW
    span = queries.shape[0]
    local_rows, width = stream.shape
    top = expert_ids.shape[1]
    meta = jnp.concatenate([expert_ids.astype(jnp.float32), gate_weights], axis=1)
    meta = jnp.pad(meta, ((0, 0), (0, 128 - 2 * top)))
    kv = jnp.concatenate([key_rows, value_rows], axis=1)
    all_kv, all_meta = gather((kv, meta), (False, True), (1, 1), high, 1)
    all_kv = all_kv.reshape(seq_count, span, -1)
    context = attend_fast(queries, all_kv)
    (all_context,) = gather((context,), (False,), (PARTS,), high, 2)
    all_context = all_context.reshape(seq_count * span, -1)
    part = lax.dot_general(
        all_context, out_weight, (((1,), (1,)), ((), ())), preferred_element_type=jnp.float32
    ).astype(jnp.bfloat16)
    part = part.reshape(seq_count, exp_count, local_rows, -1)
    mixed, normed = exchange(part, stream, norm_gain.reshape(1, -1))
    (all_normed,) = gather((normed,), (True,), (PARTS,), high, 4)
    blocks = seq_count * exp_count
    all_normed = all_normed.reshape(blocks, local_rows, width)
    local_experts = expert_in.shape[0]
    hidden_units = expert_out.shape[1]
    device = lax.axis_index("seq") * exp_count + lax.axis_index("exp")
    all_meta = all_meta.reshape(blocks, local_rows, -1)
    ids = all_meta[..., :top].astype(jnp.int32)
    gates = all_meta[..., top : 2 * top]
    here = device * local_experts + jnp.arange(local_experts, dtype=jnp.int32)
    hit = ids[:, None, :, :] == here[None, :, None, None]
    chosen = jnp.any(hit, axis=-1)
    gate = jnp.sum(jnp.where(hit, gates[:, None], 0.0), axis=-1)
    place = jnp.cumsum(chosen.astype(jnp.int32), axis=-1) - 1
    onehot = chosen[:, :, None, :] & (
        place[:, :, None, :] == jnp.arange(CAP, dtype=jnp.int32)[None, None, :, None]
    )
    slot_gate = jnp.sum(jnp.where(onehot, gate[:, :, None, :], 0.0), axis=-1)
    chooser = onehot.astype(jnp.bfloat16).reshape(blocks, local_experts * CAP, local_rows)
    arranged = (
        jnp.einsum("bsr,brd->bsd", chooser, all_normed, preferred_element_type=jnp.float32)
        .astype(jnp.bfloat16)
        .reshape(blocks, local_experts, CAP, width)
    )
    gate_up = jnp.einsum("secd,edf->secf", arranged, expert_in, preferred_element_type=jnp.float32)
    act = (jax.nn.silu(gate_up[..., :hidden_units]) * gate_up[..., hidden_units:]).astype(
        jnp.bfloat16
    )
    result = jnp.einsum("secf,efd->secd", act, expert_out, preferred_element_type=jnp.float32)
    result = (result * slot_gate[..., None]).astype(jnp.bfloat16)
    partial = jnp.einsum(
        "bsr,bsd->brd",
        chooser,
        result.reshape(blocks, local_experts * CAP, width),
        preferred_element_type=jnp.float32,
    ).astype(jnp.bfloat16)
    partial = partial.reshape(high, LOW, exp_count, local_rows, width)
    return scatter(partial, mixed, high)


def solution(mesh):
    in_specs = (
        P(("groups", "seq", "exp"), None),
        P(("groups", "seq"), "exp"),
        P(("groups", "seq"), "exp"),
        P(("groups", "seq"), "exp"),
        P("seq", "exp"),
        P(),
        P(("groups", "seq", "exp"), None),
        P(("groups", "seq", "exp"), None),
        P(("seq", "exp"), None, None),
        P(("seq", "exp"), None, None),
    )
    out_specs = P(("groups", "seq", "exp"), None)
    return jax.shard_map(
        on_device, mesh=mesh, in_specs=in_specs, out_specs=out_specs, check_vma=False
    )
```

```python
import functools

import jax
import jax.numpy as jnp
from jax import lax
from jax.experimental import pallas as pl
from jax.experimental.pallas import tpu as pltpu
from jax.sharding import PartitionSpec as P

HD = 128
EXPERTS = 64
CAP = 12
LOW = 2
PARTS = 2
VMEM_LIMIT = 67043328
neg_large = -1e30


def split_position():
    seq = lax.axis_index("seq")
    return seq // LOW, seq % LOW, lax.axis_index("exp")


def line_barrier(high, h, l, e):
    barrier = pltpu.get_barrier_semaphore()

    def greet(target):
        pl.semaphore_signal(barrier, inc=1, device_id=target, device_id_type=pl.DeviceIdType.MESH)

    @pl.when(h + 1 < high)
    def _():
        greet({"seq": (h + 1) * LOW + l})

    @pl.when(h > 0)
    def _():
        greet({"seq": (h - 1) * LOW + l})

    greet({"seq": h * LOW + 1 - l})
    greet({"exp": 1 - e})

    ends = jnp.where(h + 1 < high, 1, 0) + jnp.where(h > 0, 1, 0)
    pl.semaphore_wait(barrier, ends + 2)


def gather_steps(high, outs, cross, parts, recv, send, h, l, e):
    count = len(outs)

    def slot(a, h0, l0, e0, c):
        rows = outs[a].shape[-2] // parts[a]
        at = (h0, l0, e0) if cross[a] else (h0, l0)
        return outs[a].at[at + (pl.ds(c * rows, rows),)]

    def copy(a, h0, l0, e0, c, way):
        target = (
            {"seq": (h + 1) * LOW + l},
            {"seq": (h - 1) * LOW + l},
            {"seq": h * LOW + 1 - l},
            {"exp": 1 - e},
        )[way]
        ref = slot(a, h0, l0, e0, c)
        return pltpu.make_async_remote_copy(
            src_ref=ref,
            dst_ref=ref,
            send_sem=send[a].at[way, h0, l0, c],
            recv_sem=recv[a].at[h0, l0, e0, c],
            device_id=target,
            device_id_type=pl.DeviceIdType.MESH,
        )

    def pass_on(a, h0, c, right, left):
        if right:
            @pl.when(h + 1 < high)
            def _():
                copy(a, h0, l, e, c, 0).start()
        if left:
            @pl.when(h > 0)
            def _():
                copy(a, h0, l, e, c, 1).start()
        copy(a, h0, l, e, c, 2).start()
        if cross[a]:
            copy(a, h0, l, e, c, 3).start()

    def from_across(a, h0, c):
        copy(a, h0, 1 - l, e, c, 2).wait_recv()
        if cross[a]:
            copy(a, h0, 1 - l, e, c, 3).start()

    for a in range(count):
        for c in range(parts[a]):
            pass_on(a, h, c, True, True)
    for t in range(1, high + 1):
        if t < high:
            for a in range(count):
                for c in range(parts[a]):
                    @pl.when(h - t >= 0)
                    def _():
                        copy(a, h - t, l, e, c, 0).wait_recv()
                        pass_on(a, h - t, c, True, False)

                    @pl.when(h + t < high)
                    def _():
                        copy(a, h + t, l, e, c, 1).wait_recv()
                        pass_on(a, h + t, c, False, True)
        for a in range(count):
            for c in range(parts[a]):
                if t == 1:
                    from_across(a, h, c)
                else:
                    @pl.when(h - t + 1 >= 0)
                    def _():
                        from_across(a, h - t + 1, c)

                    @pl.when(h + t - 1 < high)
                    def _():
                        from_across(a, h + t - 1, c)
    for a in range(count):
        for c in range(parts[a]):
            for h0 in range(high):
                if cross[a]:
                    for l0 in range(LOW):
                        copy(a, h0, l0, 1 - e, c, 3).wait_recv()
                        copy(a, h0, l0, e, c, 3).wait_send()
                copy(a, h0, l, e, c, 2).wait_send()

                @pl.when((h + 1 < high) & (h0 <= h))
                def _():
                    copy(a, h0, l, e, c, 0).wait_send()

                @pl.when((h > 0) & (h0 >= h))
                def _():
                    copy(a, h0, l, e, c, 1).wait_send()


def all_barrier(high, h, l, e):
    barrier = pltpu.get_barrier_semaphore()
    mesh_id = pl.DeviceIdType.MESH
    for d in range(1, high):
        pl.semaphore_signal(
            barrier, inc=1, device_id={"seq": (h + d) % high * LOW + l}, device_id_type=mesh_id
        )
    pl.semaphore_signal(barrier, inc=1, device_id={"seq": h * LOW + 1 - l}, device_id_type=mesh_id)
    pl.semaphore_signal(barrier, inc=1, device_id={"exp": 1 - e}, device_id_type=mesh_id)
    pl.semaphore_wait(barrier, high + 1)


def attend(query_ref, kv_ref, out_ref, me):
    half = kv_ref.shape[-1] // 2
    groups = half // HD
    rows, columns = query_ref.shape
    per_group = columns // (groups * HD)
    scale = 1.0 / (HD ** 0.5)
    stacked = per_group * rows
    for g in range(groups):
        q = jnp.concatenate(
            [query_ref[:, pl.ds((g * per_group + i) * HD, HD)] for i in range(per_group)], axis=0
        )

        def piece(b, state, masked):
            largest, total, summed = state
            k = kv_ref[b // LOW, b % LOW, :, pl.ds(g * HD, HD)]
            v = kv_ref[b // LOW, b % LOW, :, pl.ds(half + g * HD, HD)]
            scores = lax.dot_general(
                q, k, (((1,), (1,)), ((), ())), preferred_element_type=jnp.float32
            ) * scale
            if masked:
                row = lax.broadcasted_iota(jnp.int32, scores.shape, 0) % rows
                column = lax.broadcasted_iota(jnp.int32, scores.shape, 1)
                scores = jnp.where(column <= row, scores, neg_large)
            new = jnp.maximum(largest, jnp.max(scores, axis=-1, keepdims=True))
            rescale = jnp.exp(largest - new)
            exps = jnp.exp(scores - new)
            total = total * rescale + jnp.sum(exps, axis=-1, keepdims=True)
            summed = summed * rescale + jnp.dot(
                exps.astype(jnp.bfloat16), v, preferred_element_type=jnp.float32
            )
            return new, total, summed

        state = (
            jnp.full((stacked, 1), neg_large, jnp.float32),
            jnp.zeros((stacked, 1), jnp.float32),
            jnp.zeros((stacked, HD), jnp.float32),
        )
        state = piece(me, state, True)
        state = lax.fori_loop(0, me, lambda b, s: piece(b, s, False), state)
        result = (state[2] / state[1]).astype(out_ref.dtype)
        for i in range(per_group):
            out_ref[:, pl.ds((g * per_group + i) * HD, HD)] = result[i * rows : (i + 1) * rows]


def front_kernel(
    high, kv_in, meta_in, query_ref, weight_in, stream_ref, gain_ref,
    mixed_ref, normed_ref, meta_all,
    kv_all, weights, context, contexts, part, mine, ready, landed,
    kv_r, meta_r, kv_s, meta_s, local, weight_sem, line_s, line_r, over_s, over_r, away_s, away_r
):
    h, l, e = split_position()
    mesh_id = pl.DeviceIdType.MESH
    copies = [
        pltpu.make_async_copy(kv_in, kv_all.at[h, l], local.at[0]),
        pltpu.make_async_copy(meta_in, meta_all.at[h, l, e], local.at[1]),
        pltpu.make_async_copy(weight_in, weights.at[l], local.at[2]),
    ]
    for one in copies:
        one.start()
    all_barrier(high, h, l, e)
    for one in copies:
        one.wait()
    gather_steps(
        high, (kv_all, meta_all), (False, True), (1, 1), (kv_r, meta_r), (kv_s, meta_s), h, l, e
    )
    weight_copy = pltpu.make_async_remote_copy(
        src_ref=weights.at[l],
        dst_ref=weights.at[l],
        send_sem=weight_sem.at[0],
        recv_sem=weight_sem.at[1],
        device_id={"seq": h * LOW + 1 - l},
        device_id_type=mesh_id,
    )
    weight_copy.start()
    attend(query_ref, kv_all, context, h * LOW + l)
    own = pltpu.make_async_copy(context, contexts.at[h], local.at[0])
    own.start()
    own.wait()
    parts = PARTS
    rows = context.shape[0] // parts

    def hop(way, h0, c):
        ref = contexts.at[h0, pl.ds(c * rows, rows)]
        return pltpu.make_async_remote_copy(
            src_ref=ref,
            dst_ref=ref,
            send_sem=line_s.at[way, h0, c],
            recv_sem=line_r.at[h0, c],
            device_id={"seq": (h + 1 - 2 * way) * LOW + l},
            device_id_type=mesh_id,
        )

    def hops(h0, c, right, left):
        if right:
            @pl.when(h + 1 < high)
            def _():
                hop(0, h0, c).start()
        if left:
            @pl.when(h > 0)
            def _():
                hop(1, h0, c).start()

    for c in range(parts):
        hops(h, c, True, True)
    for t in range(1, high):
        for c in range(parts):
            @pl.when(h - t >= 0)
            def _():
                hop(0, h - t, c).wait_recv()
                hops(h - t, c, True, False)

            @pl.when(h + t < high)
            def _():
                hop(1, h + t, c).wait_recv()
                hops(h + t, c, False, True)
    weight_back = pltpu.make_async_remote_copy(
        src_ref=weights.at[1 - l],
        dst_ref=weights.at[1 - l],
        send_sem=weight_sem.at[0],
        recv_sem=weight_sem.at[1],
        device_id={"seq": h * LOW + 1 - l},
        device_id_type=mesh_id,
    )
    weight_back.wait_recv()
    rows_e, features = part.shape[2:]
    slim = features // LOW

    def over(h0):
        return pltpu.make_async_remote_copy(
            src_ref=part.at[h0, 1 - e],
            dst_ref=mine.at[h0],
            send_sem=over_s.at[h0],
            recv_sem=over_r.at[h0],
            device_id={"exp": 1 - e},
            device_id_type=mesh_id,
        )

    def away(h0, source):
        return pltpu.make_async_remote_copy(
            src_ref=ready.at[h0],
            dst_ref=landed.at[source],
            send_sem=away_s.at[h0],
            recv_sem=away_r.at[source],
            device_id={"seq": h0 * LOW + l},
            device_id_type=mesh_id,
        )

    @pl.loop(0, high)
    def _(d):
        h0 = (h + 1 + d) % high
        for l0 in range(LOW):
            product = lax.dot_general(
                contexts[h0], weights[l0], (((1,), (1,)), ((), ())), preferred_element_type=jnp.float32
            ).astype(part.dtype)
            for e0 in range(2):
                part[h0, e0, :, pl.ds(l0 * slim, slim)] = product[e0 * rows_e : (e0 + 1) * rows_e]
        over(h0).start()

    for d in range(1, high + 1):
        h0 = (h + d) % high
        over(h0).wait_recv()
        total = part[h0, e].astype(jnp.float32) + mine[h0].astype(jnp.float32)
        ready[h0] = total.astype(ready.dtype)
        if d < high:
            away(h0, h).start()
    landed[h] = ready[h]
    for d in range(1, high):
        away((h + d) % high, (h + high - d) % high).wait_recv()
    squares = None
    for h0 in range(high):
        columns = pl.ds(h0 * features, features)
        value = stream_ref[:, columns].astype(jnp.float32) + landed[h0].astype(jnp.float32)
        mixed_ref[:, columns] = value
        term = jnp.sum(value * value, axis=-1, keepdims=True)
        squares = term if squares is None else squares + term
    factor = lax.rsqrt(squares / (high * features) + 1e-06)
    for h0 in range(high):
        columns = pl.ds(h0 * features, features)
        normed_ref[:, columns] = (mixed_ref[:, columns] * factor * gain_ref[:, columns]).astype(
            normed_ref.dtype
        )
    weight_copy.wait_send()
    for h0 in range(high):
        over(h0).wait_send()
        for c in range(parts):
            @pl.when((h + 1 < high) & (h0 <= h))
            def _():
                hop(0, h0, c).wait_send()

            @pl.when((h > 0) & (h0 >= h))
            def _():
                hop(1, h0, c).wait_send()
    for d in range(1, high):
        away((h + d) % high, h).wait_send()


def front(kv, meta, queries, weight, stream, gain, high):
    whole = pl.BlockSpec(memory_space=pltpu.VMEM)
    span = queries.shape[0]
    rows = stream.shape[0]
    features = weight.shape[0] * LOW
    kind = jnp.bfloat16
    sem = pltpu.SemaphoreType.DMA
    return pl.pallas_call(
        functools.partial(front_kernel, high),
        out_shape=(
            jax.ShapeDtypeStruct(stream.shape, jnp.float32),
            jax.ShapeDtypeStruct(stream.shape, kind),
            jax.ShapeDtypeStruct((high, LOW, 2) + meta.shape, meta.dtype),
        ),
        in_specs=[whole] * 6,
        out_specs=(whole,) * 3,
        scratch_shapes=[
            pltpu.VMEM((high, LOW) + kv.shape, kind),
            pltpu.VMEM((LOW,) + weight.shape, kind),
            pltpu.VMEM(queries.shape, kind),
            pltpu.VMEM((high,) + queries.shape, kind),
            pltpu.VMEM((high, 2, rows, features), kind),
            pltpu.VMEM((high, rows, features), kind),
            pltpu.VMEM((high, rows, features), kind),
            pltpu.VMEM((high, rows, features), kind),
            sem((high, LOW, 2, 1)),
            sem((high, LOW, 2, 1)),
            sem((4, high, LOW, 1)),
            sem((4, high, LOW, 1)),
            sem((3,)),
            sem((2,)),
            sem((2, high, PARTS)),
            sem((high, PARTS)),
            sem((high,)),
            sem((high,)),
            sem((high,)),
            sem((high,)),
        ],
        compiler_params=pltpu.CompilerParams(
            collective_id=1, has_side_effects=True, vmem_limit_bytes=VMEM_LIMIT
        ),
        name="front",
    )(kv, meta, queries, weight, stream, gain)


def back_kernel(
    high, parts, normed_ref, mixed_ref, choose_ref, combine_ref, first_hbm, second_hbm, out_ref,
    every, first, second, picked, act, near, sums, across, running, line,
    local, weight_sem, recv, send, near_s, near_r, across_s, across_r, line_s, line_r
):
    h, l, e = split_position()
    experts, width, double = first.shape
    hidden = double // 2
    slots = picked.shape[2]
    loads = []
    for i in range(experts):
        loads.append(pltpu.make_async_copy(first_hbm.at[i], first.at[i], weight_sem.at[0, i]))
        loads.append(pltpu.make_async_copy(second_hbm.at[i], second.at[i], weight_sem.at[1, i]))
    for one in loads:
        one.start()
    own = pltpu.make_async_copy(normed_ref, every.at[h, l, e], local.at[0])
    own.start()
    line_barrier(high, h, l, e)
    own.wait()
    gather_steps(high, (every,), (True,), (parts,), (recv,), (send,), h, l, e)
    for one in loads:
        one.wait()
    rows_all = every.shape[1] * every.shape[2] * every.shape[3]
    tile = 512

    @pl.loop(0, high)
    def _(h0):
        for n in range(0, width, tile):
            tokens = every[h0, :, :, :, pl.ds(n, tile)].reshape(rows_all, tile)
            value = jnp.dot(choose_ref[h0], tokens, preferred_element_type=jnp.float32)
            for i in range(experts):
                picked[i, h0, :, pl.ds(n, tile)] = value[i * slots : (i + 1) * slots].astype(
                    picked.dtype
                )

    def run(i, carry):
        step = 256
        rows = picked[i].reshape(high * slots, width)
        for f in range(0, hidden, step):
            gate = jnp.dot(rows, first[i, :, pl.ds(f, step)], preferred_element_type=jnp.float32)
            up = jnp.dot(
                rows, first[i, :, pl.ds(hidden + f, step)], preferred_element_type=jnp.float32
            )
            act[:, pl.ds(f, step)] = (gate / (1.0 + jnp.exp(-gate)) * up).astype(act.dtype)
        for n in range(0, width, tile):
            value = jnp.dot(
                act[...], second[i, :, pl.ds(n, tile)], preferred_element_type=jnp.float32
            ).astype(picked.dtype)
            picked[i, :, :, pl.ds(n, tile)] = value.reshape(high, slots, tile)
        return carry

    lax.fori_loop(0, experts, run, 0)
    scatter_steps(
        high, parts, every, mixed_ref, out_ref, near, sums, across, running, line,
        near_s, near_r, across_s, across_r, line_s, line_r, h, l, e, combine_ref, picked, tile
    )


def scatter_steps(
    high, parts, part_ref, mixed_ref, out_ref, near, sums, across, running, line,
    near_s, near_r, across_s, across_r, line_s, line_r, h, l, e, combine_ref, picked, tile
):
    rows = part_ref.shape[-2] // parts
    mesh_id = pl.DeviceIdType.MESH
    order = []
    for i in range(high):
        order.append(i // 2 if i % 2 == 0 else high - 1 - i // 2)

    def to_near(h0, l0, c):
        at = pl.ds(c * rows, rows)
        return pltpu.make_async_remote_copy(
            src_ref=part_ref.at[h0, l0, 1 - e, at],
            dst_ref=near.at[h0, l0, at],
            send_sem=near_s.at[h0, l0, c],
            recv_sem=near_r.at[h0, l0, c],
            device_id={"exp": 1 - e},
            device_id_type=mesh_id,
        )

    def to_across(h0, c):
        at = pl.ds(c * rows, rows)
        return pltpu.make_async_remote_copy(
            src_ref=sums.at[h0, at],
            dst_ref=across.at[h0, at],
            send_sem=across_s.at[h0, c],
            recv_sem=across_r.at[h0, c],
            device_id={"seq": h * LOW + 1 - l},
            device_id_type=mesh_id,
        )

    def to_line(way, h0, c):
        at = pl.ds(c * rows, rows)
        return pltpu.make_async_remote_copy(
            src_ref=running.at[h0, at],
            dst_ref=line.at[way, h0, at],
            send_sem=line_s.at[way, h0, c],
            recv_sem=line_r.at[way, h0, c],
            device_id={"seq": (h - 1 + 2 * way) * LOW + l},
            device_id_type=mesh_id,
        )

    pieces = [(h0, c) for h0 in order for c in range(parts)]
    experts, width = picked.shape[0], picked.shape[-1]
    shape = part_ref.shape[1:4]
    for h0 in order:
        for n in range(0, width, tile):
            rows_here = jnp.concatenate(
                [picked[i, h0, :, pl.ds(n, tile)] for i in range(experts)], axis=0
            )
            value = jnp.dot(combine_ref[h0], rows_here, preferred_element_type=jnp.float32)
            part_ref[h0, :, :, :, pl.ds(n, tile)] = value.astype(part_ref.dtype).reshape(
                shape + (tile,)
            )
        for c in range(parts):
            to_near(h0, 1 - l, c).start()
        for c in range(parts):
            to_near(h0, l, c).start()
    for h0, c in pieces:
        at = pl.ds(c * rows, rows)
        to_near(h0, 1 - l, c).wait_recv()
        value = part_ref[h0, 1 - l, e, at].astype(jnp.float32) + near[h0, 1 - l, at].astype(jnp.float32)
        sums[h0, at] = value.astype(sums.dtype)
        to_across(h0, c).start()
    for h0, c in pieces:
        at = pl.ds(c * rows, rows)
        to_near(h0, l, c).wait_recv()
        to_across(h0, c).wait_recv()

        def held():
            value = part_ref[h0, l, e, at].astype(jnp.float32) + near[h0, l, at].astype(jnp.float32)
            return value + across[h0, at].astype(jnp.float32)

        @pl.when(h0 < h)
        def _():
            @pl.when(h + 1 < high)
            def _():
                to_line(0, h0, c).wait_recv()
                running[h0, at] = (held() + line[0, h0, at].astype(jnp.float32)).astype(running.dtype)

            @pl.when(h + 1 >= high)
            def _():
                running[h0, at] = held().astype(running.dtype)

            to_line(0, h0, c).start()

        @pl.when(h0 > h)
        def _():
            @pl.when(h > 0)
            def _():
                to_line(1, h0, c).wait_recv()
                running[h0, at] = (held() + line[1, h0, at].astype(jnp.float32)).astype(running.dtype)

            @pl.when(h <= 0)
            def _():
                running[h0, at] = held().astype(running.dtype)

            to_line(1, h0, c).start()
    for c in range(parts):
        at = pl.ds(c * rows, rows)
        value = part_ref[h, l, e, at].astype(jnp.float32) + near[h, l, at].astype(jnp.float32)
        value = value + across[h, at].astype(jnp.float32) + mixed_ref[at, :]
        mixed_ref_sum = value

        @pl.when(h + 1 < high)
        def _():
            to_line(0, h, c).wait_recv()

        @pl.when(h + 1 >= high)
        def _():
            line[0, h, at] = jnp.zeros_like(line[0, h, at])

        @pl.when(h > 0)
        def _():
            to_line(1, h, c).wait_recv()

        @pl.when(h <= 0)
        def _():
            line[1, h, at] = jnp.zeros_like(line[1, h, at])

        value = mixed_ref_sum + line[0, h, at].astype(jnp.float32) + line[1, h, at].astype(jnp.float32)
        out_ref[at, :] = value.astype(out_ref.dtype)
    for h0, c in pieces:
        to_near(h0, l, c).wait_send()
        to_near(h0, 1 - l, c).wait_send()
        to_across(h0, c).wait_send()

        @pl.when(h0 < h)
        def _():
            to_line(0, h0, c).wait_send()

        @pl.when(h0 > h)
        def _():
            to_line(1, h0, c).wait_send()


def back(normed, mixed, choose, combine, expert_in, expert_out, high):
    rows, width = mixed.shape
    parts = PARTS
    whole = pl.BlockSpec(memory_space=pltpu.VMEM)
    away = pl.BlockSpec(memory_space=pl.ANY)
    kind = jnp.bfloat16
    sem = pltpu.SemaphoreType.DMA
    experts = expert_in.shape[0]
    slots = choose.shape[1] // experts
    return pl.pallas_call(
        functools.partial(back_kernel, high, parts),
        out_shape=jax.ShapeDtypeStruct((rows, width), kind),
        in_specs=[whole] * 4 + [away] * 2,
        out_specs=whole,
        scratch_shapes=[
            pltpu.VMEM((high, LOW, 2, rows, width), kind),
            pltpu.VMEM(expert_in.shape, kind),
            pltpu.VMEM(expert_out.shape, kind),
            pltpu.VMEM((experts, high, slots, width), kind),
            pltpu.VMEM((high * slots, expert_out.shape[1]), kind),
            pltpu.VMEM((high, LOW, rows, width), kind),
            pltpu.VMEM((high, rows, width), kind),
            pltpu.VMEM((high, rows, width), kind),
            pltpu.VMEM((high, rows, width), kind),
            pltpu.VMEM((2, high, rows, width), kind),
            sem((1,)),
            sem((2, experts)),
            sem((high, LOW, 2, parts)),
            sem((4, high, LOW, parts)),
        ]
        + [sem((high, LOW, parts))] * 2
        + [sem((high, parts))] * 2
        + [sem((2, high, parts))] * 2,
        compiler_params=pltpu.CompilerParams(
            collective_id=2, has_side_effects=True, vmem_limit_bytes=VMEM_LIMIT
        ),
        name="back",
    )(normed, mixed, choose, combine, expert_in, expert_out)


def on_device(
    stream,
    queries,
    key_rows,
    value_rows,
    out_weight,
    norm_gain,
    expert_ids,
    gate_weights,
    expert_in,
    expert_out,
):
    seq_count = lax.axis_size("seq")
    exp_count = lax.axis_size("exp")
    high = seq_count // LOW
    local_rows = stream.shape[0]
    top = expert_ids.shape[1]
    meta = jnp.concatenate([expert_ids.astype(jnp.float32), gate_weights], axis=1)
    meta = jnp.pad(meta, ((0, 0), (0, 128 - 2 * top)))
    kv = jnp.concatenate([key_rows, value_rows], axis=1)
    mixed, normed, all_meta = front(
        kv, meta, queries, out_weight, stream, norm_gain.reshape(1, -1), high
    )
    local_experts = expert_in.shape[0]
    device = lax.axis_index("seq") * exp_count + lax.axis_index("exp")
    inner = LOW * exp_count
    all_meta = all_meta.reshape(high * inner, local_rows, -1)
    ids = all_meta[..., :top].astype(jnp.int32)
    gates = all_meta[..., top : 2 * top]
    here = device * local_experts + jnp.arange(local_experts, dtype=jnp.int32)
    hit = ids[:, None, :, :] == here[None, :, None, None]
    chosen = jnp.any(hit, axis=-1)
    gate = jnp.sum(jnp.where(hit, gates[:, None], 0.0), axis=-1)
    place = jnp.cumsum(chosen.astype(jnp.int32), axis=-1) - 1
    place = jnp.where(chosen, place, -1).reshape(high, inner, local_experts, local_rows)
    gate = gate.reshape(high, inner, local_experts, local_rows)
    slot = jnp.arange(CAP, dtype=jnp.int32)
    same = jnp.eye(inner, dtype=jnp.bool_)
    choose = (
        (place.transpose(0, 2, 1, 3)[:, :, None, None, :, :] == slot[None, None, None, :, None, None])
        & same[None, None, :, None, :, None]
    ).astype(jnp.bfloat16)
    choose = choose.reshape(high, local_experts * inner * CAP, inner * local_rows)
    weigh = jnp.where(
        (place.transpose(0, 1, 3, 2)[:, :, :, :, None, None] == slot)
        & same[None, :, None, None, :, None],
        gate.transpose(0, 1, 3, 2)[:, :, :, :, None, None],
        0.0,
    ).astype(jnp.bfloat16)
    combine = weigh.reshape(high, inner * local_rows, local_experts * inner * CAP)
    return back(normed, mixed, choose, combine, expert_in, expert_out, high)


def solution(mesh):
    in_specs = (
        P(("groups", "seq", "exp"), None),
        P(("groups", "seq"), "exp"),
        P(("groups", "seq"), "exp"),
        P(("groups", "seq"), "exp"),
        P("seq", "exp"),
        P(),
        P(("groups", "seq", "exp"), None),
        P(("groups", "seq", "exp"), None),
        P(("seq", "exp"), None, None),
        P(("seq", "exp"), None, None),
    )
    out_specs = P(("groups", "seq", "exp"), None)
    return jax.shard_map(
        on_device, mesh=mesh, in_specs=in_specs, out_specs=out_specs, check_vma=False
    )
```

```python
import functools

import jax
import jax.numpy as jnp
from jax import lax
from jax.experimental import pallas as pl
from jax.experimental.pallas import tpu as pltpu
from jax.sharding import PartitionSpec as P

HD = 128
EXPERTS = 64
CAP = 12
LOW = 2
PARTS = 4
VMEM_LIMIT = 67043328
neg_large = -1e30


def split_position():
    seq = lax.axis_index("seq")
    return seq // LOW, seq % LOW, lax.axis_index("exp")


def line_barrier(high, h, l, e):
    barrier = pltpu.get_barrier_semaphore()

    def greet(target):
        pl.semaphore_signal(barrier, inc=1, device_id=target, device_id_type=pl.DeviceIdType.MESH)

    @pl.when(h + 1 < high)
    def _():
        greet({"seq": (h + 1) * LOW + l})

    @pl.when(h > 0)
    def _():
        greet({"seq": (h - 1) * LOW + l})

    greet({"seq": h * LOW + 1 - l})
    greet({"exp": 1 - e})

    ends = jnp.where(h + 1 < high, 1, 0) + jnp.where(h > 0, 1, 0)
    pl.semaphore_wait(barrier, ends + 2)


def gather_steps(high, outs, cross, parts, recv, send, h, l, e, beside=None):
    count = len(outs)

    def slot(a, h0, l0, e0, c):
        rows = outs[a].shape[-2] // parts[a]
        at = (h0, l0, e0) if cross[a] else (h0, l0)
        return outs[a].at[at + (pl.ds(c * rows, rows),)]

    def copy(a, h0, l0, e0, c, way):
        target = (
            {"seq": (h + 1) * LOW + l},
            {"seq": (h - 1) * LOW + l},
            {"seq": h * LOW + 1 - l},
            {"exp": 1 - e},
        )[way]
        ref = slot(a, h0, l0, e0, c)
        return pltpu.make_async_remote_copy(
            src_ref=ref,
            dst_ref=ref,
            send_sem=send[a].at[way, h0, l0, c],
            recv_sem=recv[a].at[h0, l0, e0, c],
            device_id=target,
            device_id_type=pl.DeviceIdType.MESH,
        )

    def pass_on(a, h0, c, right, left):
        if right:
            @pl.when(h + 1 < high)
            def _():
                copy(a, h0, l, e, c, 0).start()
        if left:
            @pl.when(h > 0)
            def _():
                copy(a, h0, l, e, c, 1).start()
        copy(a, h0, l, e, c, 2).start()
        if cross[a]:
            copy(a, h0, l, e, c, 3).start()

    def from_across(a, h0, c):
        copy(a, h0, 1 - l, e, c, 2).wait_recv()
        if cross[a]:
            copy(a, h0, 1 - l, e, c, 3).start()

    for a in range(count):
        for c in range(parts[a]):
            pass_on(a, h, c, True, True)
    if beside is not None:
        beside(0)
    for t in range(1, high + 1):
        if t < high:
            for a in range(count):
                for c in range(parts[a]):
                    @pl.when(h - t >= 0)
                    def _():
                        copy(a, h - t, l, e, c, 0).wait_recv()
                        pass_on(a, h - t, c, True, False)

                    @pl.when(h + t < high)
                    def _():
                        copy(a, h + t, l, e, c, 1).wait_recv()
                        pass_on(a, h + t, c, False, True)
        for a in range(count):
            for c in range(parts[a]):
                if t == 1:
                    from_across(a, h, c)
                else:
                    @pl.when(h - t + 1 >= 0)
                    def _():
                        from_across(a, h - t + 1, c)

                    @pl.when(h + t - 1 < high)
                    def _():
                        from_across(a, h + t - 1, c)
        if beside is not None and t < high:
            beside(t)
    for a in range(count):
        for c in range(parts[a]):
            for h0 in range(high):
                if cross[a]:
                    for l0 in range(LOW):
                        copy(a, h0, l0, 1 - e, c, 3).wait_recv()
                        copy(a, h0, l0, e, c, 3).wait_send()
                copy(a, h0, l, e, c, 2).wait_send()

                @pl.when((h + 1 < high) & (h0 <= h))
                def _():
                    copy(a, h0, l, e, c, 0).wait_send()

                @pl.when((h > 0) & (h0 >= h))
                def _():
                    copy(a, h0, l, e, c, 1).wait_send()


def all_barrier(high, h, l, e):
    barrier = pltpu.get_barrier_semaphore()
    mesh_id = pl.DeviceIdType.MESH
    for d in range(1, high):
        pl.semaphore_signal(
            barrier, inc=1, device_id={"seq": (h + d) % high * LOW + l}, device_id_type=mesh_id
        )
    pl.semaphore_signal(barrier, inc=1, device_id={"seq": h * LOW + 1 - l}, device_id_type=mesh_id)
    pl.semaphore_signal(barrier, inc=1, device_id={"exp": 1 - e}, device_id_type=mesh_id)
    pl.semaphore_wait(barrier, high + 1)


def attend(query_ref, kv_ref, out_ref, me, done):
    half = kv_ref.shape[-1] // 2
    groups = half // HD
    rows, columns = query_ref.shape
    per_group = columns // (groups * HD)
    scale = 1.0 / (HD ** 0.5)
    stacked = per_group * rows
    for g in range(groups):
        q = jnp.concatenate(
            [query_ref[:, pl.ds((g * per_group + i) * HD, HD)] for i in range(per_group)], axis=0
        )

        def piece(b, state, masked):
            largest, total, summed = state
            k = kv_ref[b // LOW, b % LOW, :, pl.ds(g * HD, HD)]
            v = kv_ref[b // LOW, b % LOW, :, pl.ds(half + g * HD, HD)]
            scores = lax.dot_general(
                q, k, (((1,), (1,)), ((), ())), preferred_element_type=jnp.float32
            ) * scale
            if masked:
                row = lax.broadcasted_iota(jnp.int32, scores.shape, 0) % rows
                column = lax.broadcasted_iota(jnp.int32, scores.shape, 1)
                scores = jnp.where(column <= row, scores, neg_large)
            new = jnp.maximum(largest, jnp.max(scores, axis=-1, keepdims=True))
            rescale = jnp.exp(largest - new)
            exps = jnp.exp(scores - new)
            total = total * rescale + jnp.sum(exps, axis=-1, keepdims=True)
            summed = summed * rescale + jnp.dot(
                exps.astype(jnp.bfloat16), v, preferred_element_type=jnp.float32
            )
            return new, total, summed

        state = (
            jnp.full((stacked, 1), neg_large, jnp.float32),
            jnp.zeros((stacked, 1), jnp.float32),
            jnp.zeros((stacked, HD), jnp.float32),
        )
        state = piece(me, state, True)
        state = lax.fori_loop(0, me, lambda b, s: piece(b, s, False), state)
        result = (state[2] / state[1]).astype(out_ref.dtype)
        for i in range(per_group):
            out_ref[:, pl.ds((g * per_group + i) * HD, HD)] = result[i * rows : (i + 1) * rows]
        done(g)


def front_kernel(
    high, key_in, value_in, ids_ref, gates_ref, query_ref, weight_in, stream_ref, gain_ref,
    mixed_ref, normed_ref, meta_all,
    kv_all, weights, context, contexts, part, mine, ready, landed,
    kv_r, meta_r, kv_s, meta_s, local, weight_sem, line_s, line_r, over_s, over_r, away_s, away_r
):
    h, l, e = split_position()
    mesh_id = pl.DeviceIdType.MESH
    half = key_in.shape[1]
    top = ids_ref.shape[1]
    copies = [
        pltpu.make_async_copy(key_in, kv_all.at[h, l, :, pl.ds(0, half)], local.at[0]),
        pltpu.make_async_copy(value_in, kv_all.at[h, l, :, pl.ds(half, half)], local.at[1]),
        pltpu.make_async_copy(weight_in, weights.at[l], local.at[2]),
    ]
    for one in copies:
        one.start()
    meta_all[h, l, e] = jnp.zeros_like(meta_all[h, l, e])
    meta_all[h, l, e, :, pl.ds(0, top)] = ids_ref[...].astype(jnp.float32)
    meta_all[h, l, e, :, pl.ds(top, top)] = gates_ref[...]
    all_barrier(high, h, l, e)
    for one in copies:
        one.wait()
    gather_steps(
        high, (kv_all, meta_all), (False, True), (2, 1), (kv_r, meta_r), (kv_s, meta_s), h, l, e
    )
    weight_copy = pltpu.make_async_remote_copy(
        src_ref=weights.at[l],
        dst_ref=weights.at[l],
        send_sem=weight_sem.at[0],
        recv_sem=weight_sem.at[1],
        device_id={"seq": h * LOW + 1 - l},
        device_id_type=mesh_id,
    )
    weight_copy.start()
    parts = half // HD
    columns = context.shape[1] // parts

    def hop(way, h0, c):
        ref = contexts.at[h0, :, pl.ds(c * columns, columns)]
        return pltpu.make_async_remote_copy(
            src_ref=ref,
            dst_ref=ref,
            send_sem=line_s.at[way, h0, c],
            recv_sem=line_r.at[h0, c],
            device_id={"seq": (h + 1 - 2 * way) * LOW + l},
            device_id_type=mesh_id,
        )

    def hops(h0, c, right, left):
        if right:
            @pl.when(h + 1 < high)
            def _():
                hop(0, h0, c).start()
        if left:
            @pl.when(h > 0)
            def _():
                hop(1, h0, c).start()

    def done(c):
        at = pl.ds(c * columns, columns)
        own = pltpu.make_async_copy(context.at[:, at], contexts.at[h, :, at], local.at[0])
        own.start()
        own.wait()
        hops(h, c, True, True)

    attend(query_ref, kv_all, context, h * LOW + l, done)
    for t in range(1, high):
        for c in range(parts):
            @pl.when(h - t >= 0)
            def _():
                hop(0, h - t, c).wait_recv()
                hops(h - t, c, True, False)

            @pl.when(h + t < high)
            def _():
                hop(1, h + t, c).wait_recv()
                hops(h + t, c, False, True)
    weight_back = pltpu.make_async_remote_copy(
        src_ref=weights.at[1 - l],
        dst_ref=weights.at[1 - l],
        send_sem=weight_sem.at[0],
        recv_sem=weight_sem.at[1],
        device_id={"seq": h * LOW + 1 - l},
        device_id_type=mesh_id,
    )
    weight_back.wait_recv()
    rows_e, features = part.shape[2:]
    slim = features // LOW

    def over(h0):
        return pltpu.make_async_remote_copy(
            src_ref=part.at[h0, 1 - e],
            dst_ref=mine.at[h0],
            send_sem=over_s.at[h0],
            recv_sem=over_r.at[h0],
            device_id={"exp": 1 - e},
            device_id_type=mesh_id,
        )

    def away(h0, source):
        return pltpu.make_async_remote_copy(
            src_ref=ready.at[h0],
            dst_ref=landed.at[source],
            send_sem=away_s.at[h0],
            recv_sem=away_r.at[source],
            device_id={"seq": h0 * LOW + l},
            device_id_type=mesh_id,
        )

    @pl.loop(0, high)
    def _(d):
        h0 = (h + 1 + d) % high
        for l0 in range(LOW):
            product = lax.dot_general(
                contexts[h0], weights[l0], (((1,), (1,)), ((), ())), preferred_element_type=jnp.float32
            ).astype(part.dtype)
            for e0 in range(2):
                part[h0, e0, :, pl.ds(l0 * slim, slim)] = product[e0 * rows_e : (e0 + 1) * rows_e]
        over(h0).start()

    for d in range(1, high + 1):
        h0 = (h + d) % high
        over(h0).wait_recv()
        total = part[h0, e].astype(jnp.float32) + mine[h0].astype(jnp.float32)
        ready[h0] = total.astype(ready.dtype)
        if d < high:
            away(h0, h).start()
    landed[h] = ready[h]
    for d in range(1, high):
        away((h + d) % high, (h + high - d) % high).wait_recv()
    squares = None
    for h0 in range(high):
        block = pl.ds(h0 * features, features)
        value = stream_ref[:, block].astype(jnp.float32) + landed[h0].astype(jnp.float32)
        mixed_ref[:, block] = value
        term = jnp.sum(value * value, axis=-1, keepdims=True)
        squares = term if squares is None else squares + term
    factor = lax.rsqrt(squares / (high * features) + 1e-06)
    for h0 in range(high):
        block = pl.ds(h0 * features, features)
        normed_ref[:, block] = (mixed_ref[:, block] * factor * gain_ref[:, block]).astype(
            normed_ref.dtype
        )
    weight_copy.wait_send()
    for h0 in range(high):
        over(h0).wait_send()
        for c in range(parts):
            @pl.when((h + 1 < high) & (h0 <= h))
            def _():
                hop(0, h0, c).wait_send()

            @pl.when((h > 0) & (h0 >= h))
            def _():
                hop(1, h0, c).wait_send()
    for d in range(1, high):
        away((h + d) % high, h).wait_send()


def front(keys, values, ids, gates, queries, weight, stream, gain, high):
    whole = pl.BlockSpec(memory_space=pltpu.VMEM)
    span = queries.shape[0]
    rows = stream.shape[0]
    features = weight.shape[0] * LOW
    kind = jnp.bfloat16
    sem = pltpu.SemaphoreType.DMA
    return pl.pallas_call(
        functools.partial(front_kernel, high),
        out_shape=(
            jax.ShapeDtypeStruct(stream.shape, jnp.float32),
            jax.ShapeDtypeStruct(stream.shape, kind),
            jax.ShapeDtypeStruct((high, LOW, 2, rows, 128), jnp.float32),
        ),
        in_specs=[whole] * 8,
        out_specs=(whole,) * 3,
        scratch_shapes=[
            pltpu.VMEM((high, LOW, span, 2 * keys.shape[1]), kind),
            pltpu.VMEM((LOW,) + weight.shape, kind),
            pltpu.VMEM(queries.shape, kind),
            pltpu.VMEM((high,) + queries.shape, kind),
            pltpu.VMEM((high, 2, rows, features), kind),
            pltpu.VMEM((high, rows, features), kind),
            pltpu.VMEM((high, rows, features), kind),
            pltpu.VMEM((high, rows, features), kind),
            sem((high, LOW, 2, 2)),
            sem((high, LOW, 2, 1)),
            sem((4, high, LOW, 2)),
            sem((4, high, LOW, 1)),
            sem((3,)),
            sem((2,)),
            sem((2, high, keys.shape[1] // HD)),
            sem((high, keys.shape[1] // HD)),
            sem((high,)),
            sem((high,)),
            sem((high,)),
            sem((high,)),
        ],
        compiler_params=pltpu.CompilerParams(
            collective_id=1, has_side_effects=True, vmem_limit_bytes=VMEM_LIMIT
        ),
        name="front",
    )(keys, values, ids, gates, queries, weight, stream, gain)


def back_kernel(
    high, parts, top, normed_ref, mixed_ref, meta_ref, first_hbm, second_hbm, out_ref,
    choose_ref, combine_ref, every, first, second, picked, act, near, sums, across, running, line,
    local, weight_sem, recv, send, near_s, near_r, across_s, across_r, line_s, line_r
):
    h, l, e = split_position()
    experts, width, double = first.shape
    hidden = double // 2
    slots = picked.shape[2]
    loads = []
    for i in range(experts):
        loads.append(pltpu.make_async_copy(first_hbm.at[i], first.at[i], weight_sem.at[0, i]))
        loads.append(pltpu.make_async_copy(second_hbm.at[i], second.at[i], weight_sem.at[1, i]))
    for one in loads:
        one.start()
    own = pltpu.make_async_copy(normed_ref, every.at[h, l, e], local.at[0])
    own.start()
    line_barrier(high, h, l, e)
    own.wait()
    device = (h * LOW + l) * 2 + e
    tokens_here, total = combine_ref.shape[1:]
    span = every.shape[3]

    def build(h0):
        meta = meta_ref[h0].reshape(tokens_here, 128)
        moved = pltpu.roll(meta, 128 - top, axis=1)
        lane = lax.broadcasted_iota(jnp.int32, meta.shape, 1)
        chosen, gates, table = [], [], jnp.zeros_like(meta)
        for i in range(experts):
            here = (device * experts + i).astype(jnp.float32)
            hit = (meta == here) & (lane < top)
            chosen.append(jnp.sum(jnp.where(hit, 1.0, 0.0), axis=1, keepdims=True))
            gates.append(jnp.sum(jnp.where(hit, moved, 0.0), axis=1, keepdims=True))
            table = table + jnp.where(lane == i, chosen[i], 0.0)
        square = (tokens_here, tokens_here)
        row = lax.broadcasted_iota(jnp.int32, square, 0)
        column = lax.broadcasted_iota(jnp.int32, square, 1)
        earlier = jnp.where((column < row) & (row // span == column // span), 1.0, 0.0)
        place = jnp.dot(
            earlier.astype(jnp.bfloat16), table.astype(jnp.bfloat16), preferred_element_type=jnp.float32
        )
        wide = (tokens_here, -(-total // 128) * 128)
        number = lax.broadcasted_iota(jnp.int32, wide, 1).astype(jnp.float32)
        block = (lax.broadcasted_iota(jnp.int32, (tokens_here, 1), 0) // span).astype(jnp.float32)
        onehot, weigh = jnp.zeros(wide, jnp.float32), jnp.zeros(wide, jnp.float32)
        for i in range(experts):
            within = jnp.sum(jnp.where(lane == i, place, 0.0), axis=1, keepdims=True)
            match = (number == within + block * CAP + i * slots) & (chosen[i] > 0.5)
            onehot = onehot + jnp.where(match, 1.0, 0.0)
            weigh = weigh + jnp.where(match, gates[i], 0.0)
        combine_ref[h0] = weigh[:, :total].astype(combine_ref.dtype)
        choose_ref[h0] = jnp.transpose(onehot)[:total].astype(choose_ref.dtype)

    gather_steps(high, (every,), (True,), (parts,), (recv,), (send,), h, l, e, build)
    for one in loads:
        one.wait()
    rows_all = every.shape[1] * every.shape[2] * every.shape[3]
    tile = 512

    @pl.loop(0, high)
    def _(h0):
        for n in range(0, width, tile):
            tokens = every[h0, :, :, :, pl.ds(n, tile)].reshape(rows_all, tile)
            value = jnp.dot(choose_ref[h0], tokens, preferred_element_type=jnp.float32)
            for i in range(experts):
                picked[i, h0, :, pl.ds(n, tile)] = value[i * slots : (i + 1) * slots].astype(
                    picked.dtype
                )

    def run(i, carry):
        step = 256
        rows = picked[i].reshape(high * slots, width)
        for f in range(0, hidden, step):
            gate = jnp.dot(rows, first[i, :, pl.ds(f, step)], preferred_element_type=jnp.float32)
            up = jnp.dot(
                rows, first[i, :, pl.ds(hidden + f, step)], preferred_element_type=jnp.float32
            )
            act[:, pl.ds(f, step)] = (gate / (1.0 + jnp.exp(-gate)) * up).astype(act.dtype)
        for n in range(0, width, tile):
            value = jnp.dot(
                act[...], second[i, :, pl.ds(n, tile)], preferred_element_type=jnp.float32
            ).astype(picked.dtype)
            picked[i, :, :, pl.ds(n, tile)] = value.reshape(high, slots, tile)
        return carry

    lax.fori_loop(0, experts, run, 0)
    scatter_steps(
        high, parts, every, mixed_ref, out_ref, near, sums, across, running, line,
        near_s, near_r, across_s, across_r, line_s, line_r, h, l, e, combine_ref, picked, tile
    )


def scatter_steps(
    high, parts, part_ref, mixed_ref, out_ref, near, sums, across, running, line,
    near_s, near_r, across_s, across_r, line_s, line_r, h, l, e, combine_ref, picked, tile
):
    rows = part_ref.shape[-2] // parts
    mesh_id = pl.DeviceIdType.MESH
    order = []
    for i in range(high):
        order.append(i // 2 if i % 2 == 0 else high - 1 - i // 2)

    def to_near(h0, l0, c):
        at = pl.ds(c * rows, rows)
        return pltpu.make_async_remote_copy(
            src_ref=part_ref.at[h0, l0, 1 - e, at],
            dst_ref=near.at[h0, l0, at],
            send_sem=near_s.at[h0, l0, c],
            recv_sem=near_r.at[h0, l0, c],
            device_id={"exp": 1 - e},
            device_id_type=mesh_id,
        )

    def to_across(h0, c):
        at = pl.ds(c * rows, rows)
        return pltpu.make_async_remote_copy(
            src_ref=sums.at[h0, at],
            dst_ref=across.at[h0, at],
            send_sem=across_s.at[h0, c],
            recv_sem=across_r.at[h0, c],
            device_id={"seq": h * LOW + 1 - l},
            device_id_type=mesh_id,
        )

    def to_line(way, h0, c):
        at = pl.ds(c * rows, rows)
        return pltpu.make_async_remote_copy(
            src_ref=running.at[h0, at],
            dst_ref=line.at[way, h0, at],
            send_sem=line_s.at[way, h0, c],
            recv_sem=line_r.at[way, h0, c],
            device_id={"seq": (h - 1 + 2 * way) * LOW + l},
            device_id_type=mesh_id,
        )

    pieces = [(h0, c) for h0 in order for c in range(parts)]
    experts, width = picked.shape[0], picked.shape[-1]
    shape = part_ref.shape[1:4]
    for h0 in order:
        for n in range(0, width, tile):
            rows_here = jnp.concatenate(
                [picked[i, h0, :, pl.ds(n, tile)] for i in range(experts)], axis=0
            )
            value = jnp.dot(combine_ref[h0], rows_here, preferred_element_type=jnp.float32)
            part_ref[h0, :, :, :, pl.ds(n, tile)] = value.astype(part_ref.dtype).reshape(
                shape + (tile,)
            )
        for c in range(parts):
            to_near(h0, 1 - l, c).start()
        for c in range(parts):
            to_near(h0, l, c).start()
    for h0, c in pieces:
        at = pl.ds(c * rows, rows)
        to_near(h0, 1 - l, c).wait_recv()
        value = part_ref[h0, 1 - l, e, at].astype(jnp.float32) + near[h0, 1 - l, at].astype(jnp.float32)
        sums[h0, at] = value.astype(sums.dtype)
        to_across(h0, c).start()
    for h0, c in pieces:
        at = pl.ds(c * rows, rows)
        to_near(h0, l, c).wait_recv()
        to_across(h0, c).wait_recv()

        def held():
            value = part_ref[h0, l, e, at].astype(jnp.float32) + near[h0, l, at].astype(jnp.float32)
            return value + across[h0, at].astype(jnp.float32)

        @pl.when(h0 < h)
        def _():
            @pl.when(h + 1 < high)
            def _():
                to_line(0, h0, c).wait_recv()
                running[h0, at] = (held() + line[0, h0, at].astype(jnp.float32)).astype(running.dtype)

            @pl.when(h + 1 >= high)
            def _():
                running[h0, at] = held().astype(running.dtype)

            to_line(0, h0, c).start()

        @pl.when(h0 > h)
        def _():
            @pl.when(h > 0)
            def _():
                to_line(1, h0, c).wait_recv()
                running[h0, at] = (held() + line[1, h0, at].astype(jnp.float32)).astype(running.dtype)

            @pl.when(h <= 0)
            def _():
                running[h0, at] = held().astype(running.dtype)

            to_line(1, h0, c).start()
    for c in range(parts):
        at = pl.ds(c * rows, rows)
        value = part_ref[h, l, e, at].astype(jnp.float32) + near[h, l, at].astype(jnp.float32)
        value = value + across[h, at].astype(jnp.float32) + mixed_ref[at, :]
        mixed_ref_sum = value

        @pl.when(h + 1 < high)
        def _():
            to_line(0, h, c).wait_recv()

        @pl.when(h + 1 >= high)
        def _():
            line[0, h, at] = jnp.zeros_like(line[0, h, at])

        @pl.when(h > 0)
        def _():
            to_line(1, h, c).wait_recv()

        @pl.when(h <= 0)
        def _():
            line[1, h, at] = jnp.zeros_like(line[1, h, at])

        value = mixed_ref_sum + line[0, h, at].astype(jnp.float32) + line[1, h, at].astype(jnp.float32)
        out_ref[at, :] = value.astype(out_ref.dtype)
    for h0, c in pieces:
        to_near(h0, l, c).wait_send()
        to_near(h0, 1 - l, c).wait_send()
        to_across(h0, c).wait_send()

        @pl.when(h0 < h)
        def _():
            to_line(0, h0, c).wait_send()

        @pl.when(h0 > h)
        def _():
            to_line(1, h0, c).wait_send()


def back(normed, mixed, meta, expert_in, expert_out, high, top):
    rows, width = mixed.shape
    parts = PARTS
    whole = pl.BlockSpec(memory_space=pltpu.VMEM)
    away = pl.BlockSpec(memory_space=pl.ANY)
    kind = jnp.bfloat16
    sem = pltpu.SemaphoreType.DMA
    experts = expert_in.shape[0]
    slots = LOW * 2 * CAP
    tokens = LOW * 2 * rows
    return pl.pallas_call(
        functools.partial(back_kernel, high, parts, top),
        out_shape=jax.ShapeDtypeStruct((rows, width), kind),
        in_specs=[whole] * 3 + [away] * 2,
        out_specs=whole,
        scratch_shapes=[
            pltpu.VMEM((high, experts * slots, tokens), kind),
            pltpu.VMEM((high, tokens, experts * slots), kind),
            pltpu.VMEM((high, LOW, 2, rows, width), kind),
            pltpu.VMEM(expert_in.shape, kind),
            pltpu.VMEM(expert_out.shape, kind),
            pltpu.VMEM((experts, high, slots, width), kind),
            pltpu.VMEM((high * slots, expert_out.shape[1]), kind),
            pltpu.VMEM((high, LOW, rows, width), kind),
            pltpu.VMEM((high, rows, width), kind),
            pltpu.VMEM((high, rows, width), kind),
            pltpu.VMEM((high, rows, width), kind),
            pltpu.VMEM((2, high, rows, width), kind),
            sem((1,)),
            sem((2, experts)),
            sem((high, LOW, 2, parts)),
            sem((4, high, LOW, parts)),
        ]
        + [sem((high, LOW, parts))] * 2
        + [sem((high, parts))] * 2
        + [sem((2, high, parts))] * 2,
        compiler_params=pltpu.CompilerParams(
            collective_id=2, has_side_effects=True, vmem_limit_bytes=VMEM_LIMIT
        ),
        name="back",
    )(normed, mixed, meta, expert_in, expert_out)


def on_device(
    stream,
    queries,
    key_rows,
    value_rows,
    out_weight,
    norm_gain,
    expert_ids,
    gate_weights,
    expert_in,
    expert_out,
):
    high = lax.axis_size("seq") // LOW
    mixed, normed, meta = front(
        key_rows, value_rows, expert_ids, gate_weights, queries, out_weight, stream,
        norm_gain.reshape(1, -1), high,
    )
    return back(normed, mixed, meta, expert_in, expert_out, high, expert_ids.shape[1])


def solution(mesh):
    in_specs = (
        P(("groups", "seq", "exp"), None),
        P(("groups", "seq"), "exp"),
        P(("groups", "seq"), "exp"),
        P(("groups", "seq"), "exp"),
        P("seq", "exp"),
        P(),
        P(("groups", "seq", "exp"), None),
        P(("groups", "seq", "exp"), None),
        P(("seq", "exp"), None, None),
        P(("seq", "exp"), None, None),
    )
    out_specs = P(("groups", "seq", "exp"), None)
    return jax.shard_map(
        on_device, mesh=mesh, in_specs=in_specs, out_specs=out_specs, check_vma=False
    )
```
